32 devices in a mesh: row: 4 (over z), col: 4 (over y, x), depth: 2 (over core).
Axes of the slice: x: 2, y: 2, z: 4, core: 2. Of those that a mesh axis runs over, the one named last changes fastest.
Arguments:
- tiles: float32 [4, 4, 96, 256, 256], P('row', 'col', 'depth'), as said below
- tile_rows: int32 [4, 4, 96], P('row', 'col', 'depth'), may hold values from 0 to 127, as said below
- tile_cols: int32 [4, 4, 96], P('row', 'col', 'depth'), may hold values from 0 to 127
- tile_count: int32 [4, 4, 2], P('row', 'col', 'depth'), may hold values from 16 to 48, as said below
Outputs:
- row_scale: float32 [131072], P('row')
- col_scale: float32 [131072], P('col')
- scaled_tiles: float32 [4, 4, 96, 256, 256], P('row', 'col', 'depth')
The draws below stay inside these ranges and needn't reach their ends.
Inputs may be any that keep to these rules, and one draw needn't show every extreme that they name: `tile_rows`: every block row and every block column of the matrix holds a live tile; no block is listed twice among the live tiles of the two depth lists of one row and col index. `tile_count`: some device's list is full in every draw. `tiles`: entries in empty slots are ignored.
All inputs are finite; a program needn't handle non-finite values.
Results may differ from the reference program's by a relative error of at most 0.0001.
Values sent between devices are 32-bit elements; how exact they have to be, the bound alone decides.
A program may use at most 128 MiB of HBM per device.

```python
import math
import jax
import jax.numpy as jnp
from jax import lax

TILE = 256
RB_DEV = 128
ANCHORS = 16
SWEEPS = 4
SLOTS = 48
CB_DEV = 128
ROW_GROUPS = 4
COL_GROUPS = 4
DEPTH_SPLIT = 2


def pattern(key):
    base_key = jax.random.fold_in(key, 7)
    key_extra, key_order, key_count = jax.random.split(base_key, 3)
    groups_row = ROW_GROUPS
    groups_col = COL_GROUPS
    depths = DEPTH_SPLIT
    row_pos = jnp.arange(groups_row, dtype=jnp.int32)[:, None, None, None]
    col_pos = jnp.arange(groups_col, dtype=jnp.int32)[None, :, None, None]
    depth_pos = jnp.arange(depths, dtype=jnp.int32)[None, None, :, None]
    anchor_ids = jnp.arange(ANCHORS, dtype=jnp.int32)[None, None, None, :]
    shape_four = (groups_row, groups_col, depths, ANCHORS)
    anchor_cols = jnp.broadcast_to((row_pos * depths + depth_pos) * ANCHORS + anchor_ids, shape_four)
    extra_cols = jax.random.randint(key_extra, (groups_row, groups_col, depths, 2 * ANCHORS), 0, CB_DEV).astype(jnp.int32)
    all_cols = jnp.concatenate([anchor_cols, extra_cols], axis=3)
    window_start = col_pos * depths * ANCHORS
    anchor_spot = jnp.broadcast_to(window_start + depth_pos * ANCHORS + anchor_ids, shape_four)
    second_spot = jnp.broadcast_to(window_start + depths * ANCHORS + depth_pos * ANCHORS + anchor_ids, shape_four)
    third_spot = jnp.broadcast_to(window_start + depths * ANCHORS + (depths + depth_pos) * ANCHORS + anchor_ids, shape_four)
    spots = jnp.concatenate([anchor_spot, second_spot, third_spot], axis=3) % RB_DEV
    order_keys = jax.random.split(key_order, groups_row)
    row_order = jax.vmap(lambda one_key: jax.random.permutation(one_key, RB_DEV))(order_keys).astype(jnp.int32)
    flat_spots = spots.reshape(groups_row, groups_col * depths * SLOTS)
    all_rows = jnp.take_along_axis(row_order, flat_spots, axis=1)
    all_rows = all_rows.reshape(groups_row, groups_col, depths * SLOTS).astype(jnp.int32)
    all_cols = all_cols.reshape(groups_row, groups_col, depths * SLOTS).astype(jnp.int32)
    level = jax.random.randint(key_count, (groups_row, groups_col, depths), 0, 2 * ANCHORS + 1).astype(jnp.int32)
    extra = level * level * level // (4 * ANCHORS * ANCHORS)
    counts = ANCHORS + extra
    chosen = jax.random.randint(jax.random.fold_in(key_count, 1), (), 0, groups_row * groups_col * depths).astype(jnp.int32)
    flat_ids = jnp.arange(groups_row * groups_col * depths, dtype=jnp.int32).reshape(groups_row, groups_col, depths)
    counts = jnp.where(flat_ids == chosen, jnp.int32(SLOTS), counts).astype(jnp.int32)
    return (all_rows, all_cols, counts)


def draw_tile_rows(key, part):
    return pattern(key)[0]


def draw_tile_cols(key, part):
    return pattern(key)[1]


def draw_tile_count(key, part):
    return pattern(key)[2]


def draw_tiles(key, part):
    key_values, key_rowscale, key_colscale = jax.random.split(jax.random.fold_in(key, 11), 3)
    shape_all = (ROW_GROUPS, COL_GROUPS, DEPTH_SPLIT * SLOTS, TILE, TILE)
    shape_rowscale = (ROW_GROUPS, COL_GROUPS, DEPTH_SPLIT * SLOTS, TILE, 1)
    shape_colscale = (ROW_GROUPS, COL_GROUPS, DEPTH_SPLIT * SLOTS, 1, TILE)
    entries = jax.random.normal(key_values, shape_all, jnp.float32)
    reach = math.log(30.0)
    row_spread = jnp.exp(jax.random.uniform(key_rowscale, shape_rowscale, jnp.float32, 0.0, reach))
    col_spread = jnp.exp(jax.random.uniform(key_colscale, shape_colscale, jnp.float32, 0.0, reach))
    return (entries * row_spread * col_spread).astype(jnp.float32)


def setup_inputs(seed: int = 0) -> dict:
    arg_keys = jax.random.split(jax.random.key(seed), 5)
    tiles = draw_tiles(jax.random.fold_in(arg_keys[4], 71), 0)
    tile_rows = draw_tile_rows(jax.random.fold_in(arg_keys[4], 71), 0)
    tile_cols = draw_tile_cols(jax.random.fold_in(arg_keys[4], 71), 0)
    tile_count = draw_tile_count(jax.random.fold_in(arg_keys[4], 71), 0)
    return dict(tiles=tiles, tile_rows=tile_rows, tile_cols=tile_cols, tile_count=tile_count)


EPS = 1e-06

def reference(tiles, tile_rows, tile_cols, tile_count):
    groups_row = ROW_GROUPS
    groups_col = COL_GROUPS
    slot_total = DEPTH_SPLIT * SLOTS
    slot_ids = jnp.arange(slot_total, dtype=jnp.int32)
    depth_of = slot_ids // SLOTS
    within = slot_ids % SLOTS
    live_mask = within[None, None, :] < tile_count[:, :, depth_of]
    global_rows = (jnp.arange(groups_row, dtype=jnp.int32)[:, None, None] * RB_DEV + tile_rows).reshape(groups_row * groups_col, slot_total)
    global_cols = (jnp.arange(groups_col, dtype=jnp.int32)[None, :, None] * CB_DEV + tile_cols).reshape(groups_row * groups_col, slot_total)
    flat_tiles = tiles.reshape(groups_row * groups_col, slot_total, TILE, TILE)
    flat_live = live_mask.reshape(groups_row * groups_col, slot_total)
    row_factor = jnp.ones((groups_row * RB_DEV, TILE), jnp.float32)
    col_factor = jnp.ones((groups_col * CB_DEV, TILE), jnp.float32)

    def partials(row_now, col_now, summed):

        def one_group(items):
            block_values, row_index, col_index, alive = items
            scaled = block_values * row_now[row_index][:, :, None] * col_now[col_index][:, None, :]
            magnitude = jnp.where(alive[:, None, None], jnp.abs(scaled), jnp.float32(0.0))
            if summed:
                return (magnitude.sum(axis=2), magnitude.sum(axis=1))
            return (magnitude.max(axis=2), magnitude.max(axis=1))
        row_part, col_part = lax.map(one_group, (flat_tiles, global_rows, global_cols, flat_live))
        row_zero = jnp.zeros((groups_row * RB_DEV, TILE), jnp.float32)
        col_zero = jnp.zeros((groups_col * CB_DEV, TILE), jnp.float32)
        if summed:
            row_total = row_zero.at[global_rows.reshape(-1)].add(row_part.reshape(-1, TILE))
            col_total = col_zero.at[global_cols.reshape(-1)].add(col_part.reshape(-1, TILE))
        else:
            row_total = row_zero.at[global_rows.reshape(-1)].max(row_part.reshape(-1, TILE))
            col_total = col_zero.at[global_cols.reshape(-1)].max(col_part.reshape(-1, TILE))
        return (row_total, col_total)
    for sweep_index in range(SWEEPS):
        row_peak, col_peak = partials(row_factor, col_factor, False)
        row_factor = row_factor * lax.rsqrt(row_peak + EPS)
        col_factor = col_factor * lax.rsqrt(col_peak + EPS)
    row_mass, col_mass = partials(row_factor, col_factor, True)
    row_factor = row_factor * lax.rsqrt(row_mass + EPS)
    col_factor = col_factor * lax.rsqrt(col_mass + EPS)

    def final_group(items):
        block_values, row_index, col_index, alive = items
        scaled = block_values * row_factor[row_index][:, :, None] * col_factor[col_index][:, None, :]
        return jnp.where(alive[:, None, None], scaled, jnp.float32(0.0))
    scaled_tiles = lax.map(final_group, (flat_tiles, global_rows, global_cols, flat_live))
    scaled_tiles = scaled_tiles.reshape(groups_row, groups_col, slot_total, TILE, TILE)
    return (row_factor.reshape(-1), col_factor.reshape(-1), scaled_tiles)
```

```python
import functools

import jax
import jax.numpy as jnp
from jax import lax
from jax.experimental import pallas as pl
from jax.experimental.pallas import tpu as pltpu
from jax.sharding import PartitionSpec as P

RB_DEV = 128
ANCHORS = 16
SWEEPS = 4
EPS = 1e-06
UNROLL = 8
LANES = 128
SUB = 8
MESH = pl.DeviceIdType.MESH
ROUNDS = SWEEPS + 1
ORD, OTH, KEEP, LAST = range(4)


def partner(axis, k):
    n = lax.axis_size(axis)
    me = lax.axis_index(axis)
    if n & (n - 1):
        return {axis: lax.rem(me + k, n)}
    to = me
    bit = 1
    while bit < n:
        if k & bit:
            to = to + bit * (1 - 2 * ((me // bit) % 2))
        bit *= 2
    return {axis: to}


def tree(op, xs):
    while len(xs) > 1:
        xs = [op(xs[i], xs[i + 1]) if i + 1 < len(xs) else xs[i] for i in range(0, len(xs), 2)]
    return xs[0]


def fold(x, summed):
    return x.sum(axis=0, keepdims=True) if summed else x.max(axis=0, keepdims=True)


def spread_rows(fac, wide):
    parts = wide.shape[0] // LANES
    for h in range(parts):
        wide[h * LANES:(h + 1) * LANES, :] = fac[pl.ds(h, LANES, stride=parts), :].T


def scale_kernel(
    count, rows, cols, tiles, keep, r_out, c_out,
    mag, mag_t, load_sem, tab_v, tab_s, tab_sem, pad, part,
    *refs,
):
    slots, size = tiles.shape[0], tiles.shape[1]
    parts = size // LANES
    live = count[0]
    f32 = jnp.float32

    def load(s):
        return pltpu.make_async_copy(tiles.at[s], keep.at[s], load_sem.at[s])

    @pl.loop(0, slots)
    def _(s):
        load(s).start()

    class Side:
        def __init__(self, place, axis, refs):
            self.place, self.axis = place, axis
            self.got, refs = refs[:ROUNDS], refs[ROUNDS:]
            (self.fac, self.wide, self.seg, self.acc, self.half, self.ptab_v, self.ptab_s,
             self.seg_s, self.seg_r, self.half_s, self.half_r, self.ptab_ss, self.ptab_rs, self.ptab_ls) = refs
            self.n = lax.axis_size(axis)
            self.blocks = self.wide.shape[1]

        def others(self):
            return range(self.n - 1, 0, -1)

        def table_copy(self, k):
            return pltpu.make_async_remote_copy(
                src_ref=tab_v.at[self.place], dst_ref=self.ptab_v.at[k - 1],
                send_sem=self.ptab_ss.at[k - 1], recv_sem=self.ptab_rs.at[k - 1],
                device_id=partner(self.axis, k), device_id_type=MESH)

        def table_down(self, k):
            return pltpu.make_async_copy(self.ptab_v.at[k - 1], self.ptab_s.at[k - 1], self.ptab_ls.at[k - 1])

        def seg_copy(self, t, k):
            return pltpu.make_async_remote_copy(
                src_ref=self.seg.at[t, pl.ds(0, slots)], dst_ref=self.got[t].at[k - 1, pl.ds(0, slots)],
                send_sem=self.seg_s.at[t, k - 1], recv_sem=self.seg_r.at[t, k - 1],
                device_id=partner(self.axis, k), device_id_type=MESH)

        def half_copy(self, t, k):
            return pltpu.make_async_remote_copy(
                src_ref=self.acc.at[t], dst_ref=self.half.at[t, k - 1],
                send_sem=self.half_s.at[t, k - 1], recv_sem=self.half_r.at[t, k - 1],
                device_id=partner("depth", k), device_id_type=MESH)

        def send(self, t):
            for k in self.others():
                self.seg_copy(t, k).start()

        def meet(self, t, op):
            for k in self.others():
                self.seg_copy(t, k).wait_recv()
            per = SUB // parts

            @pl.loop(0, self.blocks // SUB)
            def _(g):
                for j in range(SUB):
                    b = g * SUB + j
                    xs = [self.seg[t, tab_s[self.place, LAST, b]]]
                    xs += [self.got[t][k - 1, self.ptab_s[k - 1, LAST, b]] for k in range(1, self.n)]
                    at = j % per * parts
                    self.acc[t, g * (SUB // per) + j // per, at:at + parts, :] = tree(op, xs)

            for k in range(1, depths):
                self.half_copy(t, k).start()

        def update(self, t, op, widen):
            for k in range(1, depths):
                self.half_copy(t, k).wait_recv()
            value = tree(op, [self.acc[t]] + [self.half[t, k - 1] for k in range(1, depths)])
            value = value.reshape(self.fac.shape)
            now = self.fac[...]
            self.fac[...] = now * lax.rsqrt(now * value + EPS)
            if widen:
                spread_rows(self.fac, self.wide)

        def one_pass(self, t, other, values, summed):
            op = jnp.add if summed else jnp.maximum

            def body(p, run):
                s = tab_s[self.place, ORD, p]
                lane = jnp.full((SUB, LANES), tab_s[self.place, OTH, p], jnp.int32)
                total = [None] * parts
                for i in range(0, size, SUB):
                    f = jnp.take_along_axis(other.wide[i:i + SUB, :], lane, axis=1)
                    for h in range(parts):
                        v = values[s, i:i + SUB, h * LANES:(h + 1) * LANES] * f
                        total[h] = v if total[h] is None else op(total[h], v)
                now = jnp.concatenate([fold(v, summed) for v in total], axis=0)
                return self.extend(t, p, op, now, run)

            lax.fori_loop(0, slots, body, jnp.zeros((parts, LANES), f32), unroll=UNROLL)
            self.send(t)

        def extend(self, t, p, op, now, run):
            run = op(now, jnp.where(tab_s[self.place, KEEP, p] == 1, run, f32(0.0)))
            self.seg[t, p] = run
            return run

        def first_pass(self):
            def body(p, run):
                return self.extend(0, p, jnp.maximum, part[self.place, tab_s[self.place, ORD, p]], run)

            lax.fori_loop(0, slots, body, jnp.zeros((parts, LANES), f32), unroll=8)
            self.send(0)

        def finish(self):
            for t in range(ROUNDS):
                for k in self.others():
                    self.seg_copy(t, k).wait_send()
                for k in range(1, depths):
                    self.half_copy(t, k).wait_send()
            for k in self.others():
                self.table_copy(k).wait_send()

    depths = lax.axis_size("depth")
    half_refs = len(refs) // 2
    row = Side(0, "col", refs[:half_refs])
    col = Side(1, "row", refs[half_refs:])

    for side in (row, col):
        side.fac[...] = jnp.ones(side.fac.shape, f32)
        for t in range(ROUNDS):
            side.seg[t, slots] = jnp.zeros((parts, LANES), f32)
            for k in range(1, side.n):
                side.got[t][k - 1, slots] = jnp.zeros((parts, LANES), f32)

    barrier = pltpu.get_barrier_semaphore()
    greeted = 0
    for axis in ("row", "col", "depth"):
        for k in range(1, lax.axis_size(axis)):
            pl.semaphore_signal(barrier, inc=1, device_id=partner(axis, k), device_id_type=MESH)
            greeted += 1

    square = (LANES, LANES)
    down_i = lax.broadcasted_iota(jnp.int32, square, 0)
    along_i = lax.broadcasted_iota(jnp.int32, square, 1)
    pad[...] = jnp.full(pad.shape, 2 * LANES, jnp.int32)
    pad[0, :, 0:slots] = rows[...]
    pad[1, :, 0:slots] = cols[...]

    def count_of(x):
        return jnp.sum(x.astype(jnp.int32), axis=0, keepdims=True)

    for place in range(2):
        along = jnp.broadcast_to(pad[place], square)
        down = along.T
        down_other = jnp.broadcast_to(pad[1 - place], square).T
        rank = count_of((down < along) | ((down == along) & (down_i < along_i)))
        hit = jnp.broadcast_to(rank, square).T == along_i
        order = count_of(jnp.where(hit, down_i, 0))
        mine = count_of(jnp.where(hit, down, 0))
        other = count_of(jnp.where(hit, down_other, 0))
        ahead = count_of(jnp.where(jnp.broadcast_to(rank, square).T + 1 == along_i, down, 0))
        same = ((ahead == mine) & (along_i[0:1] > 0)).astype(jnp.int32)
        upto = count_of(down <= along_i)
        here = count_of(down == along_i)
        last = jnp.where(here > 0, upto - 1, slots)
        for at, line in ((ORD, order), (OTH, other), (KEEP, same), (LAST, last)):
            tab_v[place, at:at + 1, :] = line

    pl.semaphore_wait(barrier, greeted)
    for side in (row, col):
        for k in side.others():
            side.table_copy(k).start()
    down_copies = [pltpu.make_async_copy(tab_v.at[place], tab_s.at[place], tab_sem.at[place]) for place in range(2)]
    for c in down_copies:
        c.start()
    for c in down_copies:
        c.wait()

    @pl.loop(0, slots, unroll=2)
    def _(s):
        load(s).wait()
        u = jnp.where(s < live, jnp.abs(keep[s]), f32(0.0))
        mag[s] = u
        for h in range(parts):
            part[1, s, h:h + 1, :] = fold(u[:, h * LANES:(h + 1) * LANES], False)
        wide = functools.reduce(jnp.maximum, [u[:, h * LANES:(h + 1) * LANES] for h in range(parts)])
        for h in range(parts):
            part[0, s, h:h + 1, :] = fold(wide[h * LANES:(h + 1) * LANES, :].T, False)

    col.first_pass()
    row.first_pass()
    for side in (row, col):
        for k in side.others():
            side.table_copy(k).wait_recv()
            side.table_down(k).start()

    @pl.loop(0, slots, unroll=4)
    def _(s):
        mag_t[s] = mag[s].T

    for side in (row, col):
        for k in side.others():
            side.table_down(k).wait()

    for t in range(ROUNDS):
        op = jnp.add if t == SWEEPS else jnp.maximum
        pair = ((row, col, mag_t, mag), (col, row, mag, mag_t))
        for side, other, _, cross in pair if t % 2 == 0 else pair[::-1]:
            side.meet(t, op)
            side.update(t, op, t < SWEEPS)
            if t < SWEEPS:
                other.one_pass(t + 1, side, cross, t + 1 == SWEEPS)

    r_out[...] = row.fac[...]
    c_out[...] = col.fac[...]
    row.finish()
    col.finish()


def final_kernel(rows, cols, count, held, r_fac, c_fac, out, r_out, c_out, made, wide, zero, out_sem, fac_sem):
    slots, size = held.shape[0], held.shape[1]
    parts = size // LANES
    live = count[0]
    f32 = jnp.float32

    def store(s):
        return pltpu.make_async_copy(made.at[s], out.at[s], out_sem.at[s])

    facs = [
        pltpu.make_async_copy(r_fac, r_out, fac_sem.at[0]),
        pltpu.make_async_copy(c_fac, c_out, fac_sem.at[1]),
    ]
    zero[...] = jnp.zeros_like(zero)

    @pl.loop(0, slots)
    def _(s):
        @pl.when(s >= live)
        def _():
            pltpu.make_async_copy(zero, out.at[s], out_sem.at[s]).start()

    spread_rows(r_fac, wide)

    @pl.loop(0, slots)
    def _(s):
        @pl.when(s < live)
        def _():
            lane = jnp.full((SUB, LANES), rows[s], jnp.int32)
            c = [c_fac[pl.ds(cols[s] * parts + h, 1), :] for h in range(parts)]
            for i in range(0, size, SUB):
                f = jnp.take_along_axis(wide[i:i + SUB, :], lane, axis=1)
                for h in range(parts):
                    cut = slice(h * LANES, (h + 1) * LANES)
                    made[s, i:i + SUB, cut] = held[s, i:i + SUB, cut] * f * c[h]
            store(s).start()

    for c in facs:
        c.start()

    @pl.loop(0, slots)
    def _(s):
        store(s).wait()

    for c in facs:
        c.wait()


def shards(tiles, tile_rows, tile_cols, tile_count):
    values = tiles[0, 0]
    rows = tile_rows.reshape(-1)
    cols = tile_cols.reshape(-1)
    count = tile_count.reshape(-1)
    slots, size = values.shape[0], values.shape[1]
    parts = size // LANES
    n_row, n_col, depths = lax.axis_size("row"), lax.axis_size("col"), lax.axis_size("depth")
    col_blocks = n_row * depths * ANCHORS
    f32, i32 = jnp.float32, jnp.int32
    dma = pltpu.SemaphoreType.DMA
    smem = pl.BlockSpec(memory_space=pltpu.SMEM)
    vmem = pl.BlockSpec(memory_space=pltpu.VMEM)
    whole = pl.BlockSpec(memory_space=pl.ANY)

    def side_scratch(blocks, others):
        lines = blocks * parts
        dense = (lines // SUB, SUB, LANES)
        return [
            *[pltpu.VMEM((others, slots + 1, parts, LANES), f32) for _ in range(ROUNDS)],
            pltpu.VMEM((lines, LANES), f32),
            pltpu.VMEM((size, blocks), f32),
            pltpu.VMEM((ROUNDS, slots + 1, parts, LANES), f32),
            pltpu.VMEM((ROUNDS, *dense), f32),
            pltpu.VMEM((ROUNDS, depths - 1, *dense), f32),
            pltpu.VMEM((others, SUB, LANES), i32),
            pltpu.SMEM((others, SUB, LANES), i32),
            dma((ROUNDS, others)), dma((ROUNDS, others)),
            dma((ROUNDS, depths - 1)), dma((ROUNDS, depths - 1)),
            dma((others,)), dma((others,)), dma((others,)),
        ]

    held, row_scale, col_scale = pl.pallas_call(
        scale_kernel,
        out_shape=(
            pltpu.VMEM(values.shape, f32),
            pltpu.VMEM((RB_DEV * parts, LANES), f32),
            pltpu.VMEM((col_blocks * parts, LANES), f32),
        ),
        in_specs=[smem, vmem, vmem, whole],
        out_specs=(vmem, vmem, vmem),
        scratch_shapes=[
            pltpu.VMEM(values.shape, f32),
            pltpu.VMEM(values.shape, f32),
            dma((slots,)),
            pltpu.VMEM((2, SUB, LANES), i32),
            pltpu.SMEM((2, SUB, LANES), i32),
            dma((2,)),
            pltpu.VMEM((2, 1, LANES), i32),
            pltpu.VMEM((2, slots, parts, LANES), f32),
            *side_scratch(RB_DEV, n_col - 1),
            *side_scratch(col_blocks, n_row - 1),
        ],
        compiler_params=pltpu.CompilerParams(
            collective_id=0, has_side_effects=True, vmem_limit_bytes=40 * 2**20
        ),
        name="equilibrate",
    )(count, rows[None], cols[None], values)

    scaled, row_scale, col_scale = pl.pallas_call(
        final_kernel,
        in_specs=[smem, smem, smem, vmem, vmem, vmem],
        out_specs=(whole, whole, whole),
        out_shape=(
            jax.ShapeDtypeStruct(values.shape, f32),
            jax.ShapeDtypeStruct(row_scale.shape, f32),
            jax.ShapeDtypeStruct(col_scale.shape, f32),
        ),
        scratch_shapes=[
            pltpu.VMEM(values.shape, f32),
            pltpu.VMEM((size, RB_DEV), f32),
            pltpu.VMEM((size, size), f32),
            dma((slots,)),
            dma((2,)),
        ],
        compiler_params=pltpu.CompilerParams(vmem_limit_bytes=24 * 2**20),
        name="scale_tiles",
    )(rows, cols, count, held, row_scale, col_scale)
    return (row_scale.reshape(-1), col_scale.reshape(-1), scaled[None, None])


def solution(mesh):
    in_specs = (
        P("row", "col", "depth", None, None),
        P("row", "col", "depth"),
        P("row", "col", "depth"),
        P("row", "col", "depth"),
    )
    out_specs = (P("row"), P("col"), P("row", "col", "depth", None, None))
    return jax.shard_map(shards, mesh=mesh, in_specs=in_specs, out_specs=out_specs, check_vma=False)
```

```python
import functools

import jax
import jax.numpy as jnp
from jax import lax
from jax.experimental import pallas as pl
from jax.experimental.pallas import tpu as pltpu
from jax.sharding import PartitionSpec as P

RB_DEV = 128
ANCHORS = 16
SWEEPS = 4
EPS = 1e-06
UNROLL = 2
GROUP = 4
TERMS = 3
BIG = 3e38
LANES = 128
SUB = 8
MESH = pl.DeviceIdType.MESH
ROUNDS = SWEEPS + 1
ORD, OTH, KEEP, LAST, IDS = range(5)


def partner(axis, k):
    n = lax.axis_size(axis)
    me = lax.axis_index(axis)
    if n & (n - 1):
        return {axis: lax.rem(me + k, n)}
    to = me
    bit = 1
    while bit < n:
        if k & bit:
            to = to + bit * (1 - 2 * ((me // bit) % 2))
        bit *= 2
    return {axis: to}


def tree(op, xs):
    while len(xs) > 1:
        xs = [op(xs[i], xs[i + 1]) if i + 1 < len(xs) else xs[i] for i in range(0, len(xs), 2)]
    return xs[0]


def fold(x, summed):
    return x.sum(axis=0, keepdims=True) if summed else x.max(axis=0, keepdims=True)


def down(line):
    return jnp.broadcast_to(line, (LANES, line.shape[1])).T


def scale_kernel(
    count, rows, cols, tiles, keep, r_out, c_out, r_slot, c_slot,
    mag, mag_t, load_sem, tab_v, tab_s, tab_sem, pad, part,
    *refs,
):
    slots, size = tiles.shape[0], tiles.shape[1]
    lines = slots // SUB
    halves = [slice(h, h + LANES) for h in range(0, size, LANES)]
    live = count[0]
    f32, bf16 = jnp.float32, jnp.bfloat16

    def load(s):
        return pltpu.make_async_copy(tiles.at[s], keep.at[s], load_sem.at[s])

    @pl.loop(0, slots)
    def _(s):
        load(s).start()

    def thin(x, op):
        return tree(op, [x[i:i + SUB] for i in range(0, x.shape[0], SUB)])

    class Side:
        def __init__(self, place, axis, refs):
            self.place, self.axis = place, axis
            self.got, refs = refs[:ROUNDS], refs[ROUNDS:]
            (self.fac, self.seg, self.acc, self.half, self.pick, self.split, self.ptab,
             self.seg_s, self.seg_r, self.half_s, self.half_r, self.ptab_s, self.ptab_r) = refs
            self.n = lax.axis_size(axis)

        def others(self):
            return range(self.n - 1, 0, -1)

        def table_copy(self, k):
            return pltpu.make_async_remote_copy(
                src_ref=tab_v.at[self.place], dst_ref=self.ptab.at[k - 1],
                send_sem=self.ptab_s.at[k - 1], recv_sem=self.ptab_r.at[k - 1],
                device_id=partner(self.axis, k), device_id_type=MESH)

        def seg_copy(self, t, k):
            return pltpu.make_async_remote_copy(
                src_ref=self.seg.at[t], dst_ref=self.got[t].at[k - 1],
                send_sem=self.seg_s.at[t, k - 1], recv_sem=self.seg_r.at[t, k - 1],
                device_id=partner(self.axis, k), device_id_type=MESH)

        def half_copy(self, t, k):
            return pltpu.make_async_remote_copy(
                src_ref=self.acc.at[t], dst_ref=self.half.at[t, k - 1],
                send_sem=self.half_s.at[t, k - 1], recv_sem=self.half_r.at[t, k - 1],
                device_id=partner("depth", k), device_id_type=MESH)

        def send(self, t):
            for k in self.others():
                self.seg_copy(t, k).start()

        def learn(self, k, table):
            last = down(table[LAST:LAST + 1, :])
            wide = self.pick.shape[2]
            for j in range(0, wide, LANES):
                lane = lax.broadcasted_iota(jnp.int32, last.shape, 1) + j
                hit = (last == lane % slots) & (lane < TERMS * slots)
                self.pick[k, :, j:j + LANES] = hit.astype(f32).astype(bf16)

        def place_list(self, k, values):
            x = values.reshape(slots, size)
            high = jnp.minimum(x, f32(BIG)).astype(bf16)
            x = x - high.astype(f32)
            mid = x.astype(bf16)
            low = (x - mid.astype(f32)).astype(bf16)
            for i, term in enumerate((high, mid, low)):
                self.split[k, i * slots:(i + 1) * slots, :] = term
            return jnp.dot(self.pick[k], self.split[k], preferred_element_type=f32)

        def meet(self, t, op):
            xs = [self.place_list(0, self.seg[t])]
            for k in range(1, self.n):
                self.seg_copy(t, k).wait_recv()
                xs.append(self.place_list(k, self.got[t][k - 1]))
            self.acc[t] = tree(op, xs)
            for k in range(1, depths):
                self.half_copy(t, k).start()

        def update(self, t, op):
            for k in range(1, depths):
                self.half_copy(t, k).wait_recv()
            value = tree(op, [self.acc[t]] + [self.half[t, k - 1] for k in range(1, depths)])
            now = self.fac[...]
            self.fac[...] = now * lax.rsqrt(now * value + EPS)

        def run_lines(self, t, partial, op, unroll):
            def body(g, run):
                for j in range(SUB):
                    p = g * SUB + j
                    same = tab_s[self.place, KEEP, p] == 1
                    now = partial(tab_s[self.place, ORD, p], tab_s[self.place, OTH, p])
                    run = tuple(op(x, jnp.where(same, r, f32(0.0))) for x, r in zip(now, run))
                    for cut, r in zip(halves, run):
                        self.seg[t, g, j:j + 1, cut] = fold(r, op is jnp.add)
                return run

            zero = jnp.zeros((SUB, LANES), f32)
            lax.fori_loop(0, lines, body, (zero,) * len(halves), unroll=unroll)
            self.send(t)

        def one_pass(self, t, other, values, op):
            def partial(s, b):
                f = down(other.fac[pl.ds(b, 1), :])
                return [thin(values[s, :, cut] * f, op) for cut in halves]

            self.run_lines(t, partial, op, UNROLL)

        def first_pass(self):
            self.run_lines(0, lambda s, _: [part[self.place, s, :, cut] for cut in halves], jnp.maximum, 1)

        def finish(self):
            for t in range(ROUNDS):
                for k in self.others():
                    self.seg_copy(t, k).wait_send()
                for k in range(1, depths):
                    self.half_copy(t, k).wait_send()
            for k in self.others():
                self.table_copy(k).wait_send()

    depths = lax.axis_size("depth")
    half_refs = len(refs) // 2
    row = Side(0, "col", refs[:half_refs])
    col = Side(1, "row", refs[half_refs:])

    barrier = pltpu.get_barrier_semaphore()
    greeted = 0
    for axis in ("row", "col", "depth"):
        for k in range(1, lax.axis_size(axis)):
            pl.semaphore_signal(barrier, inc=1, device_id=partner(axis, k), device_id_type=MESH)
            greeted += 1

    for side in (row, col):
        side.fac[...] = jnp.ones(side.fac.shape, f32)
        side.split[...] = jnp.zeros(side.split.shape, bf16)

    square = (LANES, LANES)
    down_i = lax.broadcasted_iota(jnp.int32, square, 0)
    along_i = lax.broadcasted_iota(jnp.int32, square, 1)
    pad[...] = jnp.full(pad.shape, 2 * LANES, jnp.int32)
    pad[0, :, 0:slots] = rows[...]
    pad[1, :, 0:slots] = cols[...]

    def count_of(x):
        return jnp.sum(x.astype(jnp.int32), axis=0, keepdims=True)

    for place in range(2):
        along = jnp.broadcast_to(pad[place], square)
        ids = along.T
        other_ids = jnp.broadcast_to(pad[1 - place], square).T
        rank = count_of((ids < along) | ((ids == along) & (down_i < along_i)))
        rank = jnp.broadcast_to(rank, square).T
        hit = rank == along_i
        order = count_of(jnp.where(hit, down_i, 0))
        mine = count_of(jnp.where(hit, ids, 0))
        other = count_of(jnp.where(hit, other_ids, 0))
        ahead = count_of(jnp.where(rank + 1 == along_i, ids, 0))
        same = ((ahead == mine) & (along_i[0:1] > 0)).astype(jnp.int32)
        upto = count_of(ids <= along_i)
        here = count_of(ids == along_i)
        last = jnp.where(here > 0, upto - 1, slots)
        for at, line in ((ORD, order), (OTH, other), (KEEP, same), (LAST, last), (IDS, pad[place])):
            tab_v[place, at:at + 1, :] = line

    down_copies = [pltpu.make_async_copy(tab_v.at[place], tab_s.at[place], tab_sem.at[place]) for place in range(2)]
    for c in down_copies:
        c.start()
    for side in (row, col):
        side.learn(0, tab_v[side.place])

    group = GROUP if slots % GROUP == 0 else 1

    @pl.loop(0, slots // group)
    def _(g):
        for j in range(group):
            load(g * group + j).wait()
        for j in range(group):
            s = g * group + j
            u = jnp.where(s < live, jnp.abs(keep[s]), f32(0.0))
            mag[s] = u
            wide = functools.reduce(jnp.maximum, [u[:, cut] for cut in halves])
            for cut in halves:
                part[1, s, :, cut] = thin(u[:, cut], jnp.maximum)
                part[0, s, :, cut] = thin(wide[cut, :].T, jnp.maximum)

    for c in down_copies:
        c.wait()
    pl.semaphore_wait(barrier, greeted)
    col.first_pass()
    row.first_pass()
    for side in (row, col):
        for k in side.others():
            side.table_copy(k).start()

    @pl.loop(0, slots, unroll=4)
    def _(s):
        mag_t[s] = mag[s].T

    for side in (row, col):
        for k in side.others():
            side.table_copy(k).wait_recv()
            side.learn(k, side.ptab[k - 1])

    for t in range(ROUNDS):
        op = jnp.add if t == SWEEPS else jnp.maximum
        pair = ((row, col, mag), (col, row, mag_t))
        for side, other, cross in pair if t % 2 == 0 else pair[::-1]:
            side.meet(t, op)
            side.update(t, op)
            if t < SWEEPS:
                other.one_pass(t + 1, side, cross, jnp.add if t + 1 == SWEEPS else jnp.maximum)

    for side, out, slot in ((row, r_out, r_slot), (col, c_out, c_slot)):
        parts = len(halves)
        for h, cut in enumerate(halves):
            out[pl.ds(h, side.fac.shape[0], stride=parts), :] = side.fac[:, cut]

        @pl.loop(0, lines)
        def _(g):
            for j in range(SUB):
                s = g * SUB + j
                line = side.fac[pl.ds(tab_s[side.place, IDS, s], 1), :]
                slot[g, j:j + 1, :] = jnp.where(s < live, line, f32(0.0))

    row.finish()
    col.finish()


def final_kernel(held, r_fac, c_fac, r_slot, c_slot, out, r_out, c_out, made, out_sem, fac_sem):
    slots, size = held.shape[0], held.shape[1]

    def store(s):
        return pltpu.make_async_copy(made.at[s], out.at[s], out_sem.at[s])

    facs = [
        pltpu.make_async_copy(r_fac, r_out, fac_sem.at[0]),
        pltpu.make_async_copy(c_fac, c_out, fac_sem.at[1]),
    ]

    @pl.loop(0, slots // SUB)
    def _(g):
        for j in range(SUB):
            s = g * SUB + j
            r = down(r_slot[g, j:j + 1, :])
            c = c_slot[g, j:j + 1, :]
            for h in range(0, size, LANES):
                made[s, :, h:h + LANES] = held[s, :, h:h + LANES] * r * c[:, h:h + LANES]
            store(s).start()

    for c in facs:
        c.start()

    @pl.loop(0, slots)
    def _(s):
        store(s).wait()

    for c in facs:
        c.wait()


def shards(tiles, tile_rows, tile_cols, tile_count):
    values = tiles[0, 0]
    rows = tile_rows.reshape(1, -1)
    cols = tile_cols.reshape(1, -1)
    count = tile_count.reshape(-1)
    slots, size = values.shape[0], values.shape[1]
    parts, lines = size // LANES, slots // SUB
    n_row, n_col, depths = lax.axis_size("row"), lax.axis_size("col"), lax.axis_size("depth")
    col_blocks = n_row * depths * ANCHORS
    f32, i32, bf16 = jnp.float32, jnp.int32, jnp.bfloat16
    dma = pltpu.SemaphoreType.DMA
    smem = pl.BlockSpec(memory_space=pltpu.SMEM)
    vmem = pl.BlockSpec(memory_space=pltpu.VMEM)
    whole = pl.BlockSpec(memory_space=pl.ANY)
    terms = pl.cdiv(TERMS * slots, LANES) * LANES

    def side_scratch(blocks, others):
        return [
            *[pltpu.VMEM((others, lines, SUB, size), f32) for _ in range(ROUNDS)],
            pltpu.VMEM((blocks, size), f32),
            pltpu.VMEM((ROUNDS, lines, SUB, size), f32),
            pltpu.VMEM((ROUNDS, blocks, size), f32),
            pltpu.VMEM((ROUNDS, depths - 1, blocks, size), f32),
            pltpu.VMEM((others + 1, blocks, terms), bf16),
            pltpu.VMEM((others + 1, terms, size), bf16),
            pltpu.VMEM((others, SUB, LANES), i32),
            dma((ROUNDS, others)), dma((ROUNDS, others)),
            dma((ROUNDS, depths - 1)), dma((ROUNDS, depths - 1)),
            dma((others,)), dma((others,)),
        ]

    held, *factors = pl.pallas_call(
        scale_kernel,
        out_shape=(
            pltpu.VMEM(values.shape, f32),
            pltpu.VMEM((RB_DEV * parts, LANES), f32),
            pltpu.VMEM((col_blocks * parts, LANES), f32),
            pltpu.VMEM((lines, SUB, size), f32),
            pltpu.VMEM((lines, SUB, size), f32),
        ),
        in_specs=[smem, vmem, vmem, whole],
        out_specs=(vmem,) * 5,
        scratch_shapes=[
            pltpu.VMEM(values.shape, f32),
            pltpu.VMEM(values.shape, f32),
            dma((slots,)),
            pltpu.VMEM((2, SUB, LANES), i32),
            pltpu.SMEM((2, SUB, LANES), i32),
            dma((2,)),
            pltpu.VMEM((2, 1, LANES), i32),
            pltpu.VMEM((2, slots, SUB, size), f32),
            *side_scratch(RB_DEV, n_col - 1),
            *side_scratch(col_blocks, n_row - 1),
        ],
        compiler_params=pltpu.CompilerParams(
            collective_id=0, has_side_effects=True, vmem_limit_bytes=46 * 2**20
        ),
        name="equilibrate",
    )(count, rows, cols, values)

    scaled, row_scale, col_scale = pl.pallas_call(
        final_kernel,
        in_specs=[vmem] * 5,
        out_specs=(whole, whole, whole),
        out_shape=(
            jax.ShapeDtypeStruct(values.shape, f32),
            jax.ShapeDtypeStruct(factors[0].shape, f32),
            jax.ShapeDtypeStruct(factors[1].shape, f32),
        ),
        scratch_shapes=[
            pltpu.VMEM(values.shape, f32),
            dma((slots,)),
            dma((2,)),
        ],
        compiler_params=pltpu.CompilerParams(vmem_limit_bytes=24 * 2**20),
        name="scale_tiles",
    )(held, *factors)
    return (row_scale.reshape(-1), col_scale.reshape(-1), scaled[None, None])


def solution(mesh):
    in_specs = (
        P("row", "col", "depth", None, None),
        P("row", "col", "depth"),
        P("row", "col", "depth"),
        P("row", "col", "depth"),
    )
    out_specs = (P("row"), P("col"), P("row", "col", "depth", None, None))
    return jax.shard_map(shards, mesh=mesh, in_specs=in_specs, out_specs=out_specs, check_vma=False)
```

```python
import functools

import jax
import jax.numpy as jnp
from jax import lax
from jax.experimental import pallas as pl
from jax.experimental.pallas import tpu as pltpu
from jax.sharding import PartitionSpec as P

RB_DEV = 128
ANCHORS = 16
SWEEPS = 4
EPS = 1e-06
UNROLL = 6
GROUP = 4
TERMS = 3
BIG = 3e38
LANES = 128
SUB = 8
MESH = pl.DeviceIdType.MESH
ROUNDS = SWEEPS + 1
ORD, OTH, KEEP, LAST, IDS = range(5)


def partner(axis, k):
    n = lax.axis_size(axis)
    me = lax.axis_index(axis)
    if n & (n - 1):
        return {axis: lax.rem(me + k, n)}
    to = me
    bit = 1
    while bit < n:
        if k & bit:
            to = to + bit * (1 - 2 * ((me // bit) % 2))
        bit *= 2
    return {axis: to}


def tree(op, xs):
    while len(xs) > 1:
        xs = [op(xs[i], xs[i + 1]) if i + 1 < len(xs) else xs[i] for i in range(0, len(xs), 2)]
    return xs[0]


def fold(x, summed):
    return x.sum(axis=0, keepdims=True) if summed else x.max(axis=0, keepdims=True)


def down(line):
    return jnp.broadcast_to(line, (LANES, line.shape[1])).T


def scale_kernel(
    count, rows, cols, tiles, keep, r_out, c_out, r_slot, c_slot,
    mag, mag_t, load_sem, tab_v, tab_s, tab_sem, pad, part,
    *refs,
):
    slots, size = tiles.shape[0], tiles.shape[1]
    lines = slots // SUB
    halves = [slice(h, h + LANES) for h in range(0, size, LANES)]
    live = count[0]
    f32, bf16 = jnp.float32, jnp.bfloat16

    def load(s):
        return pltpu.make_async_copy(tiles.at[s], keep.at[s], load_sem.at[s])

    @pl.loop(0, slots)
    def _(s):
        load(s).start()

    def thin(x, op):
        return tree(op, [x[i:i + SUB] for i in range(0, x.shape[0], SUB)])

    class Side:
        def __init__(self, place, axis, refs):
            self.place, self.axis = place, axis
            self.got, refs = refs[:ROUNDS], refs[ROUNDS:]
            (self.fac, self.seg, self.acc, self.half, self.pick, self.split, self.ptab,
             self.seg_s, self.seg_r, self.half_s, self.half_r, self.ptab_s, self.ptab_r) = refs
            self.n = lax.axis_size(axis)

        def others(self):
            return range(self.n - 1, 0, -1)

        def table_copy(self, k):
            return pltpu.make_async_remote_copy(
                src_ref=tab_v.at[self.place], dst_ref=self.ptab.at[k - 1],
                send_sem=self.ptab_s.at[k - 1], recv_sem=self.ptab_r.at[k - 1],
                device_id=partner(self.axis, k), device_id_type=MESH)

        def seg_copy(self, t, k):
            return pltpu.make_async_remote_copy(
                src_ref=self.seg.at[t], dst_ref=self.got[t].at[k - 1],
                send_sem=self.seg_s.at[t, k - 1], recv_sem=self.seg_r.at[t, k - 1],
                device_id=partner(self.axis, k), device_id_type=MESH)

        def half_copy(self, t, k):
            return pltpu.make_async_remote_copy(
                src_ref=self.acc.at[t], dst_ref=self.half.at[t, k - 1],
                send_sem=self.half_s.at[t, k - 1], recv_sem=self.half_r.at[t, k - 1],
                device_id=partner("depth", k), device_id_type=MESH)

        def send(self, t):
            for k in self.others():
                self.seg_copy(t, k).start()

        def learn(self, k, table):
            last = down(table[LAST:LAST + 1, :])
            wide = self.pick.shape[2]
            for j in range(0, wide, LANES):
                lane = lax.broadcasted_iota(jnp.int32, last.shape, 1) + j
                hit = (last == lane % slots) & (lane < TERMS * slots)
                self.pick[k, :, j:j + LANES] = hit.astype(f32).astype(bf16)

        def place_list(self, k, values):
            x = values.reshape(slots, size)
            high = jnp.minimum(x, f32(BIG)).astype(bf16)
            x = x - high.astype(f32)
            mid = x.astype(bf16)
            low = (x - mid.astype(f32)).astype(bf16)
            for i, term in enumerate((high, mid, low)):
                self.split[k, i * slots:(i + 1) * slots, :] = term
            return jnp.dot(self.pick[k], self.split[k], preferred_element_type=f32)

        def meet(self, t, op):
            xs = [self.place_list(0, self.seg[t])]
            for k in range(1, self.n):
                self.seg_copy(t, k).wait_recv()
                xs.append(self.place_list(k, self.got[t][k - 1]))
            self.acc[t] = tree(op, xs)
            for k in range(1, depths):
                self.half_copy(t, k).start()

        def update(self, t, op):
            for k in range(1, depths):
                self.half_copy(t, k).wait_recv()
            value = tree(op, [self.acc[t]] + [self.half[t, k - 1] for k in range(1, depths)])
            now = self.fac[...]
            self.fac[...] = now * lax.rsqrt(now * value + EPS)

        def run_lines(self, t, partial, op, unroll):
            def body(g, run):
                for j in range(SUB):
                    p = g * SUB + j
                    same = tab_s[self.place, KEEP, p] == 1
                    now = partial(tab_s[self.place, ORD, p], tab_s[self.place, OTH, p])
                    run = tuple(op(x, jnp.where(same, r, f32(0.0))) for x, r in zip(now, run))
                    for cut, r in zip(halves, run):
                        self.seg[t, g, j:j + 1, cut] = fold(r, op is jnp.add)
                return run

            zero = jnp.zeros((SUB, LANES), f32)
            lax.fori_loop(0, lines, body, (zero,) * len(halves), unroll=unroll)
            self.send(t)

        def one_pass(self, t, other, values, op):
            def partial(s, b):
                f = down(other.fac[pl.ds(b, 1), :])
                return [thin(values[s, :, cut] * f, op) for cut in halves]

            self.run_lines(t, partial, op, UNROLL)

        def first_pass(self):
            self.run_lines(0, lambda s, _: [part[self.place, s, :, cut] for cut in halves], jnp.maximum, 1)

        def finish(self):
            for t in range(ROUNDS):
                for k in self.others():
                    self.seg_copy(t, k).wait_send()
                for k in range(1, depths):
                    self.half_copy(t, k).wait_send()
            for k in self.others():
                self.table_copy(k).wait_send()

    depths = lax.axis_size("depth")
    half_refs = len(refs) // 2
    row = Side(0, "col", refs[:half_refs])
    col = Side(1, "row", refs[half_refs:])

    barrier = pltpu.get_barrier_semaphore()
    greeted = 0
    for axis in ("row", "col", "depth"):
        for k in range(1, lax.axis_size(axis)):
            pl.semaphore_signal(barrier, inc=1, device_id=partner(axis, k), device_id_type=MESH)
            greeted += 1

    for side in (row, col):
        side.fac[...] = jnp.ones(side.fac.shape, f32)
        side.split[...] = jnp.zeros(side.split.shape, bf16)

    square = (LANES, LANES)
    down_i = lax.broadcasted_iota(jnp.int32, square, 0)
    along_i = lax.broadcasted_iota(jnp.int32, square, 1)
    pad[...] = jnp.full(pad.shape, 2 * LANES, jnp.int32)
    pad[0, :, 0:slots] = rows[...]
    pad[1, :, 0:slots] = cols[...]

    def count_of(x):
        return jnp.sum(x.astype(jnp.int32), axis=0, keepdims=True)

    for place in range(2):
        along = jnp.broadcast_to(pad[place], square)
        ids = along.T
        other_ids = jnp.broadcast_to(pad[1 - place], square).T
        rank = count_of((ids < along) | ((ids == along) & (down_i < along_i)))
        rank = jnp.broadcast_to(rank, square).T
        hit = rank == along_i
        order = count_of(jnp.where(hit, down_i, 0))
        mine = count_of(jnp.where(hit, ids, 0))
        other = count_of(jnp.where(hit, other_ids, 0))
        ahead = count_of(jnp.where(rank + 1 == along_i, ids, 0))
        same = ((ahead == mine) & (along_i[0:1] > 0)).astype(jnp.int32)
        upto = count_of(ids <= along_i)
        here = count_of(ids == along_i)
        last = jnp.where(here > 0, upto - 1, slots)
        for at, line in ((ORD, order), (OTH, other), (KEEP, same), (LAST, last), (IDS, pad[place])):
            tab_v[place, at:at + 1, :] = line

    down_copies = [pltpu.make_async_copy(tab_v.at[place], tab_s.at[place], tab_sem.at[place]) for place in range(2)]
    for c in down_copies:
        c.start()
    for side in (row, col):
        side.learn(0, tab_v[side.place])

    group = GROUP if slots % GROUP == 0 else 1

    @pl.loop(0, slots // group)
    def _(g):
        for j in range(group):
            load(g * group + j).wait()
        for j in range(group):
            s = g * group + j
            u = jnp.where(s < live, jnp.abs(keep[s]), f32(0.0))
            mag[s] = u
            wide = functools.reduce(jnp.maximum, [u[:, cut] for cut in halves])
            for cut in halves:
                part[1, s, :, cut] = thin(u[:, cut], jnp.maximum)
                part[0, s, :, cut] = thin(wide[cut, :].T, jnp.maximum)

    for c in down_copies:
        c.wait()
    pl.semaphore_wait(barrier, greeted)
    col.first_pass()
    row.first_pass()
    for side in (row, col):
        for k in side.others():
            side.table_copy(k).start()

    @pl.loop(0, slots, unroll=4)
    def _(s):
        mag_t[s] = mag[s].T

    for side in (row, col):
        for k in side.others():
            side.table_copy(k).wait_recv()
            side.learn(k, side.ptab[k - 1])

    for t in range(ROUNDS):
        op = jnp.add if t == SWEEPS else jnp.maximum
        pair = ((row, col, mag), (col, row, mag_t))
        for side, other, cross in pair[::-1] if t % 2 == 0 else pair:
            side.meet(t, op)
            side.update(t, op)
            if t < SWEEPS:
                other.one_pass(t + 1, side, cross, jnp.add if t + 1 == SWEEPS else jnp.maximum)

    for side, out, slot in ((row, r_out, r_slot), (col, c_out, c_slot)):
        parts = len(halves)
        for h, cut in enumerate(halves):
            out[pl.ds(h, side.fac.shape[0], stride=parts), :] = side.fac[:, cut]

        @pl.loop(0, lines)
        def _(g):
            for j in range(SUB):
                s = g * SUB + j
                line = side.fac[pl.ds(tab_s[side.place, IDS, s], 1), :]
                slot[g, j:j + 1, :] = jnp.where(s < live, line, f32(0.0))

    row.finish()
    col.finish()


def final_kernel(held, r_fac, c_fac, r_slot, c_slot, out, r_out, c_out, made, out_sem, fac_sem):
    slots, size = held.shape[0], held.shape[1]

    def store(s):
        return pltpu.make_async_copy(made.at[s], out.at[s], out_sem.at[s])

    facs = [
        pltpu.make_async_copy(r_fac, r_out, fac_sem.at[0]),
        pltpu.make_async_copy(c_fac, c_out, fac_sem.at[1]),
    ]

    @pl.loop(0, slots // SUB)
    def _(g):
        for j in range(SUB):
            s = g * SUB + j
            r = down(r_slot[g, j:j + 1, :])
            c = c_slot[g, j:j + 1, :]
            for h in range(0, size, LANES):
                made[s, :, h:h + LANES] = held[s, :, h:h + LANES] * r * c[:, h:h + LANES]
            store(s).start()

    for c in facs:
        c.start()

    @pl.loop(0, slots)
    def _(s):
        store(s).wait()

    for c in facs:
        c.wait()


def shards(tiles, tile_rows, tile_cols, tile_count):
    values = tiles[0, 0]
    rows = tile_rows.reshape(1, -1)
    cols = tile_cols.reshape(1, -1)
    count = tile_count.reshape(-1)
    slots, size = values.shape[0], values.shape[1]
    parts, lines = size // LANES, slots // SUB
    n_row, n_col, depths = lax.axis_size("row"), lax.axis_size("col"), lax.axis_size("depth")
    col_blocks = n_row * depths * ANCHORS
    f32, i32, bf16 = jnp.float32, jnp.int32, jnp.bfloat16
    dma = pltpu.SemaphoreType.DMA
    smem = pl.BlockSpec(memory_space=pltpu.SMEM)
    vmem = pl.BlockSpec(memory_space=pltpu.VMEM)
    whole = pl.BlockSpec(memory_space=pl.ANY)
    terms = pl.cdiv(TERMS * slots, LANES) * LANES

    def side_scratch(blocks, others):
        return [
            *[pltpu.VMEM((others, lines, SUB, size), f32) for _ in range(ROUNDS)],
            pltpu.VMEM((blocks, size), f32),
            pltpu.VMEM((ROUNDS, lines, SUB, size), f32),
            pltpu.VMEM((ROUNDS, blocks, size), f32),
            pltpu.VMEM((ROUNDS, depths - 1, blocks, size), f32),
            pltpu.VMEM((others + 1, blocks, terms), bf16),
            pltpu.VMEM((others + 1, terms, size), bf16),
            pltpu.VMEM((others, SUB, LANES), i32),
            dma((ROUNDS, others)), dma((ROUNDS, others)),
            dma((ROUNDS, depths - 1)), dma((ROUNDS, depths - 1)),
            dma((others,)), dma((others,)),
        ]

    held, *factors = pl.pallas_call(
        scale_kernel,
        out_shape=(
            pltpu.VMEM(values.shape, f32),
            pltpu.VMEM((RB_DEV * parts, LANES), f32),
            pltpu.VMEM((col_blocks * parts, LANES), f32),
            pltpu.VMEM((lines, SUB, size), f32),
            pltpu.VMEM((lines, SUB, size), f32),
        ),
        in_specs=[smem, vmem, vmem, whole],
        out_specs=(vmem,) * 5,
        scratch_shapes=[
            pltpu.VMEM(values.shape, f32),
            pltpu.VMEM(values.shape, f32),
            dma((slots,)),
            pltpu.VMEM((2, SUB, LANES), i32),
            pltpu.SMEM((2, SUB, LANES), i32),
            dma((2,)),
            pltpu.VMEM((2, 1, LANES), i32),
            pltpu.VMEM((2, slots, SUB, size), f32),
            *side_scratch(RB_DEV, n_col - 1),
            *side_scratch(col_blocks, n_row - 1),
        ],
        compiler_params=pltpu.CompilerParams(
            collective_id=0, has_side_effects=True, vmem_limit_bytes=46 * 2**20
        ),
        name="equilibrate",
    )(count, rows, cols, values)

    scaled, row_scale, col_scale = pl.pallas_call(
        final_kernel,
        in_specs=[vmem] * 5,
        out_specs=(whole, whole, whole),
        out_shape=(
            jax.ShapeDtypeStruct(values.shape, f32),
            jax.ShapeDtypeStruct(factors[0].shape, f32),
            jax.ShapeDtypeStruct(factors[1].shape, f32),
        ),
        scratch_shapes=[
            pltpu.VMEM(values.shape, f32),
            dma((slots,)),
            dma((2,)),
        ],
        compiler_params=pltpu.CompilerParams(vmem_limit_bytes=24 * 2**20),
        name="scale_tiles",
    )(held, *factors)
    return (row_scale.reshape(-1), col_scale.reshape(-1), scaled[None, None])


def solution(mesh):
    in_specs = (
        P("row", "col", "depth", None, None),
        P("row", "col", "depth"),
        P("row", "col", "depth"),
        P("row", "col", "depth"),
    )
    out_specs = (P("row"), P("col"), P("row", "col", "depth", None, None))
    return jax.shard_map(shards, mesh=mesh, in_specs=in_specs, out_specs=out_specs, check_vma=False)
```

```python
import functools

import jax
import jax.numpy as jnp
from jax import lax
from jax.experimental import pallas as pl
from jax.experimental.pallas import tpu as pltpu
from jax.sharding import PartitionSpec as P

RB_DEV = 128
ANCHORS = 16
SWEEPS = 4
EPS = 1e-06
UNROLL = 6
GROUP = 4
TERMS = 3
BIG = 3e38
SCHEDULE = ("mMuU", "muMU")
LANES = 128
SUB = 8
MESH = pl.DeviceIdType.MESH
ROUNDS = SWEEPS + 1
ORD, OTH, KEEP, LAST, IDS = range(5)


def partner(axis, k):
    n = lax.axis_size(axis)
    me = lax.axis_index(axis)
    if n & (n - 1):
        return {axis: lax.rem(me + k, n)}
    to = me
    bit = 1
    while bit < n:
        if k & bit:
            to = to + bit * (1 - 2 * ((me // bit) % 2))
        bit *= 2
    return {axis: to}


def tree(op, xs):
    while len(xs) > 1:
        xs = [op(xs[i], xs[i + 1]) if i + 1 < len(xs) else xs[i] for i in range(0, len(xs), 2)]
    return xs[0]


def fold(x, summed):
    return x.sum(axis=0, keepdims=True) if summed else x.max(axis=0, keepdims=True)


def down(line):
    return jnp.broadcast_to(line, (LANES, line.shape[1])).T


def scale_kernel(
    count, rows, cols, tiles, keep, r_out, c_out, r_slot, c_slot,
    mag, mag_t, load_sem, tab_v, tab_s, tab_sem, pad, part, rows_v, cols_v, count_s, small_sem,
    *refs,
):
    slots, size = tiles.shape[0], tiles.shape[1]
    lines = slots // SUB
    halves = [slice(h, h + LANES) for h in range(0, size, LANES)]
    f32, bf16 = jnp.float32, jnp.bfloat16

    small = [
        pltpu.make_async_copy(a, b, small_sem.at[i])
        for i, (a, b) in enumerate(((count, count_s), (rows, rows_v), (cols, cols_v)))
    ]
    for c in small:
        c.start()

    def load(s):
        return pltpu.make_async_copy(tiles.at[s], keep.at[s], load_sem.at[s])

    @pl.loop(0, slots)
    def _(s):
        load(s).start()

    def thin(x, op):
        return tree(op, [x[i:i + SUB] for i in range(0, x.shape[0], SUB)])

    class Side:
        def __init__(self, place, axis, refs):
            self.place, self.axis = place, axis
            self.got, refs = refs[:ROUNDS], refs[ROUNDS:]
            (self.fac, self.seg, self.acc, self.half, self.pick, self.split, self.ptab,
             self.seg_s, self.seg_r, self.half_s, self.half_r, self.ptab_s, self.ptab_r) = refs
            self.n = lax.axis_size(axis)

        def others(self):
            return range(self.n - 1, 0, -1)

        def table_copy(self, k):
            return pltpu.make_async_remote_copy(
                src_ref=tab_v.at[self.place], dst_ref=self.ptab.at[k - 1],
                send_sem=self.ptab_s.at[k - 1], recv_sem=self.ptab_r.at[k - 1],
                device_id=partner(self.axis, k), device_id_type=MESH)

        def seg_copy(self, t, k):
            return pltpu.make_async_remote_copy(
                src_ref=self.seg.at[t], dst_ref=self.got[t].at[k - 1],
                send_sem=self.seg_s.at[t, k - 1], recv_sem=self.seg_r.at[t, k - 1],
                device_id=partner(self.axis, k), device_id_type=MESH)

        def half_copy(self, t, k):
            return pltpu.make_async_remote_copy(
                src_ref=self.acc.at[t], dst_ref=self.half.at[t, k - 1],
                send_sem=self.half_s.at[t, k - 1], recv_sem=self.half_r.at[t, k - 1],
                device_id=partner("depth", k), device_id_type=MESH)

        def send(self, t):
            for k in self.others():
                self.seg_copy(t, k).start()

        def learn(self, k, table):
            last = down(table[LAST:LAST + 1, :])
            wide = self.pick.shape[2]
            for j in range(0, wide, LANES):
                lane = lax.broadcasted_iota(jnp.int32, last.shape, 1) + j
                hit = (last == lane % slots) & (lane < TERMS * slots)
                self.pick[k, :, j:j + LANES] = hit.astype(f32).astype(bf16)

        def place_list(self, k, values):
            x = values.reshape(slots, size)
            high = jnp.minimum(x, f32(BIG)).astype(bf16)
            x = x - high.astype(f32)
            mid = x.astype(bf16)
            low = (x - mid.astype(f32)).astype(bf16)
            for i, term in enumerate((high, mid, low)):
                self.split[k, i * slots:(i + 1) * slots, :] = term
            return jnp.dot(self.pick[k], self.split[k], preferred_element_type=f32)

        def meet(self, t, op):
            xs = [self.place_list(0, self.seg[t])]
            for k in range(1, self.n):
                self.seg_copy(t, k).wait_recv()
                xs.append(self.place_list(k, self.got[t][k - 1]))
            self.acc[t] = tree(op, xs)
            for k in range(1, depths):
                self.half_copy(t, k).start()

        def update(self, t, op):
            for k in range(1, depths):
                self.half_copy(t, k).wait_recv()
            value = tree(op, [self.acc[t]] + [self.half[t, k - 1] for k in range(1, depths)])
            now = self.fac[...]
            self.fac[...] = now * lax.rsqrt(now * value + EPS)

        def run_lines(self, t, partial, op, unroll):
            def body(g, run):
                for j in range(SUB):
                    p = g * SUB + j
                    same = tab_s[self.place, KEEP, p] == 1
                    now = partial(tab_s[self.place, ORD, p], tab_s[self.place, OTH, p])
                    run = tuple(op(x, jnp.where(same, r, f32(0.0))) for x, r in zip(now, run))
                    for cut, r in zip(halves, run):
                        self.seg[t, g, j:j + 1, cut] = fold(r, op is jnp.add)
                return run

            zero = jnp.zeros((SUB, LANES), f32)
            lax.fori_loop(0, lines, body, (zero,) * len(halves), unroll=unroll)
            self.send(t)

        def one_pass(self, t, other, values, op):
            def partial(s, b):
                f = down(other.fac[pl.ds(b, 1), :])
                return [thin(values[s, :, cut] * f, op) for cut in halves]

            self.run_lines(t, partial, op, UNROLL)

        def first_pass(self):
            self.run_lines(0, lambda s, _: [part[self.place, s, :, cut] for cut in halves], jnp.maximum, 1)

        def finish(self):
            for t in range(ROUNDS):
                for k in self.others():
                    self.seg_copy(t, k).wait_send()
                for k in range(1, depths):
                    self.half_copy(t, k).wait_send()
            for k in self.others():
                self.table_copy(k).wait_send()

    depths = lax.axis_size("depth")
    half_refs = len(refs) // 2
    row = Side(0, "col", refs[:half_refs])
    col = Side(1, "row", refs[half_refs:])

    barrier = pltpu.get_barrier_semaphore()
    greeted = 0
    for axis in ("row", "col", "depth"):
        for k in range(1, lax.axis_size(axis)):
            pl.semaphore_signal(barrier, inc=1, device_id=partner(axis, k), device_id_type=MESH)
            greeted += 1

    for side in (row, col):
        side.fac[...] = jnp.ones(side.fac.shape, f32)
        side.split[...] = jnp.zeros(side.split.shape, bf16)

    square = (LANES, LANES)
    down_i = lax.broadcasted_iota(jnp.int32, square, 0)
    along_i = lax.broadcasted_iota(jnp.int32, square, 1)
    pad[...] = jnp.full(pad.shape, 2 * LANES, jnp.int32)
    for c in small:
        c.wait()
    live = count_s[0, 0, 0]
    pad[0, :, 0:slots] = rows_v[...]
    pad[1, :, 0:slots] = cols_v[...]

    def count_of(x):
        return jnp.sum(x.astype(jnp.int32), axis=0, keepdims=True)

    for place in range(2):
        along = jnp.broadcast_to(pad[place], square)
        ids = along.T
        other_ids = jnp.broadcast_to(pad[1 - place], square).T
        rank = count_of((ids < along) | ((ids == along) & (down_i < along_i)))
        rank = jnp.broadcast_to(rank, square).T
        hit = rank == along_i
        order = count_of(jnp.where(hit, down_i, 0))
        mine = count_of(jnp.where(hit, ids, 0))
        other = count_of(jnp.where(hit, other_ids, 0))
        ahead = count_of(jnp.where(rank + 1 == along_i, ids, 0))
        same = ((ahead == mine) & (along_i[0:1] > 0)).astype(jnp.int32)
        upto = count_of(ids <= along_i)
        here = count_of(ids == along_i)
        last = jnp.where(here > 0, upto - 1, slots)
        for at, line in ((ORD, order), (OTH, other), (KEEP, same), (LAST, last), (IDS, pad[place])):
            tab_v[place, at:at + 1, :] = line

    down_copies = [pltpu.make_async_copy(tab_v.at[place], tab_s.at[place], tab_sem.at[place]) for place in range(2)]
    for c in down_copies:
        c.start()
    for side in (row, col):
        side.learn(0, tab_v[side.place])

    group = GROUP if slots % GROUP == 0 else 1

    @pl.loop(0, slots // group)
    def _(g):
        for j in range(group):
            load(g * group + j).wait()
        for j in range(group):
            s = g * group + j
            u = jnp.where(s < live, jnp.abs(keep[s]), f32(0.0))
            mag[s] = u
            wide = functools.reduce(jnp.maximum, [u[:, cut] for cut in halves])
            for cut in halves:
                part[1, s, :, cut] = thin(u[:, cut], jnp.maximum)
                part[0, s, :, cut] = thin(wide[cut, :].T, jnp.maximum)

    for c in down_copies:
        c.wait()
    pl.semaphore_wait(barrier, greeted)
    col.first_pass()
    row.first_pass()
    for side in (row, col):
        for k in side.others():
            side.table_copy(k).start()

    @pl.loop(0, slots, unroll=4)
    def _(s):
        mag_t[s] = mag[s].T

    for side in (row, col):
        for k in side.others():
            side.table_copy(k).wait_recv()
            side.learn(k, side.ptab[k - 1])

    for t in range(ROUNDS):
        op = jnp.add if t == SWEEPS else jnp.maximum
        pair = ((row, col, mag), (col, row, mag_t))
        next_op = jnp.add if t + 1 == SWEEPS else jnp.maximum
        first, second = pair[::-1] if t % 2 == 0 else pair
        for stage in SCHEDULE[min(t, len(SCHEDULE) - 1)]:
            side, other, cross = first if stage.islower() else second
            if stage.lower() == "m":
                side.meet(t, op)
            else:
                side.update(t, op)
                if t < SWEEPS:
                    other.one_pass(t + 1, side, cross, next_op)

    for side, out, slot in ((row, r_out, r_slot), (col, c_out, c_slot)):
        parts = len(halves)
        for h, cut in enumerate(halves):
            out[pl.ds(h, side.fac.shape[0], stride=parts), :] = side.fac[:, cut]

        @pl.loop(0, lines)
        def _(g):
            for j in range(SUB):
                s = g * SUB + j
                line = side.fac[pl.ds(tab_s[side.place, IDS, s], 1), :]
                slot[g, j:j + 1, :] = jnp.where(s < live, line, f32(0.0))

    row.finish()
    col.finish()


def final_kernel(held, r_fac, c_fac, r_slot, c_slot, out, r_out, c_out, made, out_sem, fac_sem):
    slots, size = held.shape[0], held.shape[1]

    def store(s):
        return pltpu.make_async_copy(made.at[s], out.at[s], out_sem.at[s])

    facs = [
        pltpu.make_async_copy(r_fac, r_out, fac_sem.at[0]),
        pltpu.make_async_copy(c_fac, c_out, fac_sem.at[1]),
    ]

    @pl.loop(0, slots // SUB)
    def _(g):
        for j in range(SUB):
            s = g * SUB + j
            r = down(r_slot[g, j:j + 1, :])
            c = c_slot[g, j:j + 1, :]
            for h in range(0, size, LANES):
                made[s, :, h:h + LANES] = held[s, :, h:h + LANES] * r * c[:, h:h + LANES]
            store(s).start()

    for c in facs:
        c.start()

    @pl.loop(0, slots)
    def _(s):
        store(s).wait()

    for c in facs:
        c.wait()


def shards(tiles, tile_rows, tile_cols, tile_count):
    values = tiles[0, 0]
    rows = tile_rows.reshape(1, -1)
    cols = tile_cols.reshape(1, -1)
    slots, size = values.shape[0], values.shape[1]
    parts, lines = size // LANES, slots // SUB
    n_row, n_col, depths = lax.axis_size("row"), lax.axis_size("col"), lax.axis_size("depth")
    col_blocks = n_row * depths * ANCHORS
    f32, i32, bf16 = jnp.float32, jnp.int32, jnp.bfloat16
    dma = pltpu.SemaphoreType.DMA
    vmem = pl.BlockSpec(memory_space=pltpu.VMEM)
    whole = pl.BlockSpec(memory_space=pl.ANY)
    terms = pl.cdiv(TERMS * slots, LANES) * LANES

    def side_scratch(blocks, others):
        return [
            *[pltpu.VMEM((others, lines, SUB, size), f32) for _ in range(ROUNDS)],
            pltpu.VMEM((blocks, size), f32),
            pltpu.VMEM((ROUNDS, lines, SUB, size), f32),
            pltpu.VMEM((ROUNDS, blocks, size), f32),
            pltpu.VMEM((ROUNDS, depths - 1, blocks, size), f32),
            pltpu.VMEM((others + 1, blocks, terms), bf16),
            pltpu.VMEM((others + 1, terms, size), bf16),
            pltpu.VMEM((others, SUB, LANES), i32),
            dma((ROUNDS, others)), dma((ROUNDS, others)),
            dma((ROUNDS, depths - 1)), dma((ROUNDS, depths - 1)),
            dma((others,)), dma((others,)),
        ]

    held, *factors = pl.pallas_call(
        scale_kernel,
        out_shape=(
            pltpu.VMEM(values.shape, f32),
            pltpu.VMEM((RB_DEV * parts, LANES), f32),
            pltpu.VMEM((col_blocks * parts, LANES), f32),
            pltpu.VMEM((lines, SUB, size), f32),
            pltpu.VMEM((lines, SUB, size), f32),
        ),
        in_specs=[pl.BlockSpec(memory_space=pltpu.HBM)] * 3 + [whole],
        out_specs=(vmem,) * 5,
        scratch_shapes=[
            pltpu.VMEM(values.shape, f32),
            pltpu.VMEM(values.shape, f32),
            dma((slots,)),
            pltpu.VMEM((2, SUB, LANES), i32),
            pltpu.SMEM((2, SUB, LANES), i32),
            dma((2,)),
            pltpu.VMEM((2, 1, LANES), i32),
            pltpu.VMEM((2, slots, SUB, size), f32),
            pltpu.VMEM((1, slots), i32),
            pltpu.VMEM((1, slots), i32),
            pltpu.SMEM((1, 1, 1), i32),
            dma((3,)),
            *side_scratch(RB_DEV, n_col - 1),
            *side_scratch(col_blocks, n_row - 1),
        ],
        compiler_params=pltpu.CompilerParams(
            collective_id=0, has_side_effects=True, vmem_limit_bytes=46 * 2**20
        ),
        name="equilibrate",
    )(tile_count, rows, cols, values)

    scaled, row_scale, col_scale = pl.pallas_call(
        final_kernel,
        in_specs=[vmem] * 5,
        out_specs=(whole, whole, whole),
        out_shape=(
            jax.ShapeDtypeStruct(values.shape, f32),
            jax.ShapeDtypeStruct(factors[0].shape, f32),
            jax.ShapeDtypeStruct(factors[1].shape, f32),
        ),
        scratch_shapes=[
            pltpu.VMEM(values.shape, f32),
            dma((slots,)),
            dma((2,)),
        ],
        compiler_params=pltpu.CompilerParams(vmem_limit_bytes=24 * 2**20),
        name="scale_tiles",
    )(held, *factors)
    return (row_scale.reshape(-1), col_scale.reshape(-1), scaled[None, None])


def solution(mesh):
    in_specs = (
        P("row", "col", "depth", None, None),
        P("row", "col", "depth"),
        P("row", "col", "depth"),
        P("row", "col", "depth"),
    )
    out_specs = (P("row"), P("col"), P("row", "col", "depth", None, None))
    return jax.shard_map(shards, mesh=mesh, in_specs=in_specs, out_specs=out_specs, check_vma=False)
```
